32 devices in a mesh: layer: 8 (over z, y), cuts: 4 (over x, core).
Axes of the slice: x: 2, y: 2, z: 4, core: 2. Of those that a mesh axis runs over, the one named last changes fastest.
Arguments:
- resid: bfloat16 [512, 2, 16384], P(None, None, 'cuts'), may hold values from -6 to 6
- enc_weight: bfloat16 [2, 16384, 2048], P(None, 'cuts', 'layer'), may hold values from -0.03125 to 0.03125
- enc_bias: float32 [2048], P('layer'), may hold values from -1 to 1
- dec_weight: bfloat16 [2048, 2, 16384], P('layer', None, 'cuts'), may hold values from -0.1875 to 0.1875
- dec_bias: float32 [2, 16384], P(None, 'cuts'), may hold values from -1 to 1
Outputs:
- enc_grad: bfloat16 [2, 16384, 2048], P(None, 'cuts', 'layer')
- dec_grad: bfloat16 [2048, 2, 16384], P('layer', None, 'cuts')
The draws below stay inside these ranges and needn't reach their ends.
All inputs are finite; a program needn't handle non-finite values.
Results may differ from the reference program's by a relative error of at most 0.012.
Values may be sent and summed in bfloat16 or wider, within the bound.
No kernel may reach another device: no remote copies, remote signals or barrier semaphores. Data moves between devices by JAX's collectives and lax.ppermute only.
A program may use at most 128 MiB of HBM per device.

```python
import jax
import jax.numpy as jnp

D = 16384
TOKENS = 512
LAYERS = 2
FEATURES = 2048


def block_scale(key, dims, pieces, least, largest):
    def one(axis_at, blocks):
        steps = jax.random.uniform(jax.random.fold_in(jax.random.fold_in(key, 6), axis_at), (blocks,), jnp.float32, least / len(pieces), largest / len(pieces))
        return jnp.repeat(jnp.exp(steps), dims[axis_at] // blocks).reshape((-1,) + (1,) * (len(dims) - axis_at - 1))

    loudness = one(*pieces[0])
    for cut in pieces[1:]:
        loudness = loudness * one(*cut)
    return loudness


def gaussian(key, extent, deviation, bound, split=(), held_as=jnp.bfloat16):
    values = jax.random.normal(key, extent, jnp.float32) * deviation
    if len(split) > 0:
        values = block_scale(key, extent, split, -0.22, 0.18) * values
    return jnp.clip(values, min=-bound, max=bound).astype(held_as)


def setup_inputs(seed: int = 0) -> dict:
    streams_of = jax.random.split(jax.random.key(seed), 6)
    return {
        "resid": gaussian(streams_of[0], (TOKENS, LAYERS, D), 1.0, 6.0, ((2, 4),)),
        "enc_weight": gaussian(streams_of[1], (LAYERS, D, FEATURES), (LAYERS * D) ** -0.5, 0.03125, ((1, 4), (2, 8))),
        "enc_bias": jnp.clip(jax.random.uniform(streams_of[2], (FEATURES,), jnp.float32, -1.0, 1.0) * block_scale(streams_of[2], (FEATURES,), ((0, 8),), -0.4, 0.0), -1.0, 1.0),
        "dec_weight": gaussian(streams_of[3], (FEATURES, LAYERS, D), (FEATURES // 2) ** -0.5, 0.1875, ((0, 8), (2, 4))),
        "dec_bias": jnp.clip(jax.random.uniform(streams_of[4], (LAYERS, D), jnp.float32, -1.0, 1.0) * block_scale(streams_of[4], (LAYERS, D), ((1, 4),), -0.4, 0.0), -1.0, 1.0),
    }


def reference(resid, enc_weight, enc_bias, dec_weight, dec_bias):
    rows = resid.shape[0]
    flat = resid.reshape(rows, -1)
    encoder = enc_weight.reshape(flat.shape[1], -1)
    decoder = dec_weight.reshape(encoder.shape[1], -1)
    scale = 1.0 / jnp.sqrt(jnp.float32(rows))
    z = jnp.dot(flat, encoder, preferred_element_type=jnp.float32) + enc_bias[None, :]
    act = jnp.maximum(z, 0.0).astype(jnp.bfloat16)
    recon = jnp.dot(act, decoder, preferred_element_type=jnp.float32)
    err = (recon + dec_bias.reshape(1, -1) - flat.astype(jnp.float32)).astype(jnp.bfloat16)
    dec_grad = (jnp.dot(act.T, err, preferred_element_type=jnp.float32) * scale).astype(jnp.bfloat16)
    dact = jnp.dot(err, decoder.T, preferred_element_type=jnp.float32) * scale
    dz = jnp.where(z > 0, dact, 0.0).astype(jnp.bfloat16)
    enc_grad = jnp.dot(flat.T, dz, preferred_element_type=jnp.float32).astype(jnp.bfloat16)
    return (enc_grad.reshape(enc_weight.shape), dec_grad.reshape(dec_weight.shape))
```

```python
import math

import jax
import jax.numpy as jnp
from jax import lax
from jax.sharding import PartitionSpec as P

F32 = jnp.float32
BF16 = jnp.bfloat16


def swap(value, axis, bit):
    size = lax.axis_size(axis)
    return lax.ppermute(value, axis, [(i, i ^ (1 << bit)) for i in range(size)])


def halves(value, upper):
    half = value.shape[0] // 2
    low, high = value[:half], value[half:]
    return jnp.where(upper, high, low), jnp.where(upper, low, high)


def joined(mine, theirs, upper):
    return jnp.where(
        upper,
        jnp.concatenate([theirs, mine], 0),
        jnp.concatenate([mine, theirs], 0),
    )


def dot(a, b, dims):
    return lax.dot_general(a, b, (dims, ((), ())), preferred_element_type=F32)


def per_device(resid, enc_weight, enc_bias, dec_weight, dec_bias):
    tokens, layers, width = resid.shape
    feats = enc_weight.shape[2]
    scale = 1.0 / math.sqrt(tokens)
    n_cuts = lax.axis_size("cuts")
    bits = n_cuts.bit_length() - 1
    line = lax.axis_size("layer") // 2
    spot = lax.axis_index("layer")
    pos, side = spot // 2, spot % 2
    cut = lax.axis_index("cuts")
    ups = [(cut >> b) % 2 == 1 for b in range(bits)]
    half = width // 2
    pieces = 2 if half // line >= 256 else 1
    span = half // pieces
    part = span // line
    cols = layers * part

    keep = lax.dynamic_slice_in_dim(dec_weight, side * half, half, 2)
    give = lax.dynamic_slice_in_dim(dec_weight, (1 - side) * half, half, 2)
    got = [swap(give[:, :, k * span : (k + 1) * span], "layer", 0) for k in range(pieces)]

    z = dot(resid.reshape(tokens, -1), enc_weight.reshape(-1, feats), ((1,), (0,)))
    for b in range(bits):
        stay, go = halves(z, ups[b])
        z = stay + swap(go, "cuts", b)
    act_mine = jnp.maximum(z + enc_bias[None, :], 0.0).astype(BF16)
    act = jnp.concatenate([act_mine, swap(act_mine, "layer", 0)], 1)
    for b in reversed(range(bits)):
        act = joined(act, swap(act, "cuts", b), ups[b])

    def shift(value, step, sources):
        pairs = [
            (2 * i + s, 2 * (i + step) + s)
            for i in sources
            if 0 <= i + step < line
            for s in range(2)
        ]
        return lax.ppermute(value, "layer", pairs)

    dact = jnp.zeros((tokens, 2 * feats), F32)
    own_grads, far_grads = [], []
    for k in range(pieces):
        both = jnp.concatenate([keep[:, :, k * span : (k + 1) * span], got[k]], 0)
        both = both.reshape(2 * feats, layers, line, part)
        both = both.transpose(2, 0, 1, 3).reshape(line, 2 * feats, cols)

        def weights(o):
            return lax.dynamic_index_in_dim(both, o, 0, keepdims=False)

        def recon(o):
            return dot(act, weights(o), ((1,), (0,)))

        start = side * half + k * span + pos * part
        right = left = None
        for s in range(1, line):
            r = recon(jnp.minimum(pos + line - s, line - 1))
            l = recon(jnp.maximum(pos - line + s, 0))
            if right is not None:
                r = r + right.astype(F32)
                l = l + left.astype(F32)
            right = shift(r.astype(BF16), 1, range(0, s))
            left = shift(l.astype(BF16), -1, range(line - s, line))
        goal = lax.dynamic_slice_in_dim(resid, start, part, 2).reshape(tokens, cols)
        offset = lax.dynamic_slice_in_dim(dec_bias, start, part, 1).reshape(1, cols)
        err = recon(pos) + right.astype(F32) + left.astype(F32)
        err = (err + offset - goal.astype(F32)).astype(BF16)

        own = jnp.zeros((line, feats, cols), BF16)
        far = jnp.zeros((line, feats, cols), BF16)

        def use(e, o, valid, own, far, dact):
            grad = (dot(act, e, ((0,), (0,))) * scale).astype(BF16)
            back = swap(grad[feats:], "layer", 0)
            if valid is None:
                own = lax.dynamic_update_index_in_dim(own, grad[:feats], o, 0)
                far = lax.dynamic_update_index_in_dim(far, back, o, 0)
            else:
                old = lax.dynamic_index_in_dim(own, o, 0, keepdims=False)
                own = lax.dynamic_update_index_in_dim(
                    own, jnp.where(valid, grad[:feats], old), o, 0
                )
                old = lax.dynamic_index_in_dim(far, o, 0, keepdims=False)
                far = lax.dynamic_update_index_in_dim(
                    far, jnp.where(valid, back, old), o, 0
                )
            return own, far, dact + dot(e, weights(o), ((1,), (1,)))

        own, far, dact = use(err, pos, None, own, far, dact)
        right = left = err
        for s in range(1, line):
            right = shift(right, 1, range(s - 1, line - 1))
            left = shift(left, -1, range(1, line - s + 1))
            from_left, from_right = pos >= s, pos + s <= line - 1
            if 2 * s < line:
                own, far, dact = use(
                    right, jnp.maximum(pos - s, 0), from_left, own, far, dact
                )
                own, far, dact = use(
                    left, jnp.minimum(pos + s, line - 1), from_right, own, far, dact
                )
            else:
                own, far, dact = use(
                    jnp.where(from_left, right, left),
                    jnp.where(from_left, pos - s, jnp.minimum(pos + s, line - 1)),
                    from_left | from_right,
                    own,
                    far,
                    dact,
                )
        own_grads.append(own)
        far_grads.append(far)

    def spread(grads):
        grads = jnp.stack(grads, 0).reshape(pieces, line, feats, layers, part)
        return grads.transpose(2, 3, 0, 1, 4).reshape(feats, layers, half)

    near, away = spread(own_grads), spread(far_grads)
    dec_grad = jnp.where(
        side == 1,
        jnp.concatenate([away, near], 2),
        jnp.concatenate([near, away], 2),
    )

    for b in range(bits):
        stay, go = halves(dact, ups[b])
        dact = stay + swap(go.astype(BF16), "cuts", b).astype(F32)
    dact = dact[:, :feats] + swap(dact[:, feats:].astype(BF16), "layer", 0).astype(F32)
    dz = jnp.where(act_mine > 0, dact * scale, 0.0).astype(BF16)
    for b in reversed(range(bits)):
        dz = joined(dz, swap(dz, "cuts", b), ups[b])
    enc_grad = dot(resid.reshape(tokens, -1), dz, ((0,), (0,)))
    return enc_grad.astype(BF16).reshape(enc_weight.shape), dec_grad


def solution(mesh):
    placed = (
        P(None, None, "cuts"),
        P(None, "cuts", "layer"),
        P("layer"),
        P("layer", None, "cuts"),
        P(None, "cuts"),
    )
    return jax.shard_map(
        per_device,
        mesh=mesh,
        in_specs=placed,
        out_specs=(P(None, "cuts", "layer"), P("layer", None, "cuts")),
        check_vma=False,
    )
```

```python
import functools
import math

import jax
import jax.numpy as jnp
import numpy as np
from jax import lax
from jax.experimental import pallas as pl
from jax.experimental.pallas import tpu as pltpu
from jax.sharding import PartitionSpec as P


F32 = jnp.float32
BF16 = jnp.bfloat16
ENDS = 1
CHAINS = 2
FLATS = 4


def swap(value, axis, bit):
    size = lax.axis_size(axis)
    return lax.ppermute(value, axis, [(i, i ^ (1 << bit)) for i in range(size)])


def halves(value, upper):
    half = value.shape[0] // 2
    low, high = value[:half], value[half:]
    return jnp.where(upper, high, low), jnp.where(upper, low, high)


def joined(mine, theirs, upper):
    return jnp.where(
        upper,
        jnp.concatenate([theirs, mine], 0),
        jnp.concatenate([mine, theirs], 0),
    )


def dot(a, b, dims):
    return lax.dot_general(a, b, (dims, ((), ())), preferred_element_type=F32)


def limits(mib):
    return pltpu.CompilerParams(vmem_limit_bytes=mib << 20)


def cost(flops, moved):
    return pl.CostEstimate(flops=flops, bytes_accessed=moved, transcendentals=0)


def enc_grad_kernel(*refs):
    *rows, dz, out = refs
    left = jnp.concatenate([r[0] for r in rows], 0)
    out[0] = dot(left, dz[...], ((0,), (0,))).astype(out.dtype)


def enc_grad_of(rows, dz, blocks):
    layers, size, width = rows[0].shape
    tokens, feats = dz.shape
    block = width // blocks
    return pl.pallas_call(
        enc_grad_kernel,
        grid=(layers, blocks),
        in_specs=[pl.BlockSpec((1, size, block), lambda l, i: (l, 0, i)) for _ in rows]
        + [pl.BlockSpec(dz.shape, lambda l, i: (0, 0))],
        out_specs=pl.BlockSpec((1, block, feats), lambda l, i: (l, i, 0)),
        out_shape=jax.ShapeDtypeStruct((layers, width, feats), BF16),
        compiler_params=limits(24),
        cost_estimate=cost(
            2 * tokens * layers * width * feats, 2 * layers * width * (tokens + feats)
        ),
    )(*rows, dz)


def prep_kernel(table, rows, out):
    _, units, feats, cols = out.shape
    layers = rows.shape[1]
    part = cols // layers
    size = feats * layers
    to = lax.broadcasted_iota(jnp.int32, (size, size), 0)
    at = lax.broadcasted_iota(jnp.int32, (size, size), 1)
    order = jnp.where(at == layers * (to % feats) + to // feats, 1.0, 0.0).astype(BF16)
    flat = rows[...].reshape(size, units * part)
    flat = dot(order, flat, ((1,), (0,))).astype(BF16)
    for u in range(units):
        for layer in range(layers):
            out[0, u, :, layer * part : (layer + 1) * part] = flat[
                layer * feats : (layer + 1) * feats, u * part : (u + 1) * part
            ]


def prep(weight, table, at, count, span, units, room=16):
    feats, layers, _ = weight.shape
    cols = layers * span // units
    return pl.pallas_call(
        prep_kernel,
        grid_spec=pltpu.PrefetchScalarGridSpec(
            num_scalar_prefetch=1,
            grid=(count,),
            in_specs=[
                pl.BlockSpec((feats, layers, span), lambda i, t: (0, 0, t[at + i]))
            ],
            out_specs=pl.BlockSpec((1, units, feats, cols), lambda i, t: (i, 0, 0, 0)),
        ),
        out_shape=jax.ShapeDtypeStruct((count, units, feats, cols), BF16),
        compiler_params=limits(room),
        cost_estimate=cost(0, 4 * count * feats * layers * span),
    )(table, weight)


def place_kernel(starts, table, *refs):
    out = refs[-1]
    part = out.shape[2]
    step = pl.program_id(0)
    for j in range(len(starts) - 1):

        @pl.when((step >= starts[j]) & (step < starts[j + 1]))
        def _(ref=refs[j]):
            for layer in range(out.shape[1]):
                out[:, layer, :] = ref[0, :, layer * part : (layer + 1) * part]


def place(groups, table, at, shape, held):
    feats, layers, _ = shape
    cols = groups[0].shape[2]
    part = cols // layers
    starts = [0]
    for g in groups:
        starts.append(starts[-1] + g.shape[0])

    def spec(j):
        most = groups[j].shape[0] - 1

        def index(i, t):
            return (jnp.clip(i - starts[j], 0, most), 0, 0)

        return pl.BlockSpec((1, feats, cols), index)

    specs = [spec(j) for j in range(len(groups))]
    operands = list(groups)
    aliases = {}
    if held is not None:
        specs.append(pl.BlockSpec(memory_space=pl.ANY))
        operands.append(held)
        aliases = {len(operands): 0}
    return pl.pallas_call(
        functools.partial(place_kernel, starts),
        grid_spec=pltpu.PrefetchScalarGridSpec(
            num_scalar_prefetch=1,
            grid=(starts[-1],),
            in_specs=specs,
            out_specs=pl.BlockSpec(
                (feats, layers, part), lambda i, t: (0, 0, t[at + i])
            ),
        ),
        out_shape=jax.ShapeDtypeStruct(shape, BF16),
        input_output_aliases=aliases,
        compiler_params=limits(16),
        cost_estimate=cost(0, 4 * starts[-1] * feats * cols),
    )(table, *operands)


def goal_kernel(table, resid, bias, out):
    part = resid.shape[2]
    for layer in range(resid.shape[1]):
        rows = resid[:, layer, :].astype(F32)
        out[0, :, layer * part : (layer + 1) * part] = bias[layer][None, :] - rows


def goals_of(resid, bias, table, at, count, part):
    tokens, layers, _ = resid.shape
    return pl.pallas_call(
        goal_kernel,
        grid_spec=pltpu.PrefetchScalarGridSpec(
            num_scalar_prefetch=1,
            grid=(count,),
            in_specs=[
                pl.BlockSpec((tokens, layers, part), lambda i, t: (0, 0, t[at + i])),
                pl.BlockSpec((layers, part), lambda i, t: (0, t[at + i])),
            ],
            out_specs=pl.BlockSpec((1, tokens, layers * part), lambda i, t: (i, 0, 0)),
        ),
        out_shape=jax.ShapeDtypeStruct((count, tokens, layers * part), F32),
        compiler_params=limits(12),
        cost_estimate=cost(0, 6 * count * tokens * layers * part),
    )(table, resid, bias)


def flat_kernel(rows, out):
    layers, count, block = out.shape
    size = count * layers
    to = lax.broadcasted_iota(jnp.int32, (size, size), 0)
    at = lax.broadcasted_iota(jnp.int32, (size, size), 1)
    order = jnp.where(at == layers * (to % count) + to // count, 1.0, 0.0).astype(BF16)
    flat = dot(order, rows[...].reshape(size, block), ((1,), (0,))).astype(BF16)
    for layer in range(layers):
        out[layer] = flat[layer * count : (layer + 1) * count]


def flat_of(resid, piece, pieces, blocks):
    tokens, layers, width = resid.shape
    size, block = tokens // pieces, width // blocks
    return pl.pallas_call(
        flat_kernel,
        grid=(blocks,),
        in_specs=[pl.BlockSpec((size, layers, block), lambda i: (piece, 0, i))],
        out_specs=pl.BlockSpec((layers, size, block), lambda i: (0, 0, i)),
        out_shape=jax.ShapeDtypeStruct((layers, size, width), BF16),
        compiler_params=limits(12),
        cost_estimate=cost(0, 4 * size * layers * width),
    )(resid)


def use_kernel(n, scale, at, has_sum, table, act_t, weights, *refs):
    errs, rest = refs[:n], refs[n:]
    near, far, total = rest[-3:]
    step = pl.program_id(0)
    base = at + 4 * step
    src, valid = table[base], table[base + 2]
    if n == 1:
        e = errs[0][...]
    else:
        e = jnp.where(src == 0, errs[0][...], errs[1][...])
        for j in range(2, n):
            e = jnp.where(src == j, errs[j][...], e)
    feats, layers, part = near.shape
    grad = (dot(act_t[...], e, ((1,), (0,))) * scale).astype(BF16)
    for layer in range(layers):
        near[:, layer, :] = grad[:feats, layer * part : (layer + 1) * part]
    far[0] = grad[feats:]
    more = dot(e, weights[0], ((1,), (1,))) * valid.astype(F32)

    @pl.when(step == 0)
    def _():
        total[...] = rest[0][...] + more if has_sum else more

    @pl.when(step > 0)
    def _():
        total[...] += more


def use_of(act_t, weights, errs, total, held, table, at, m, shape, scale):
    feats, layers, _ = shape
    _, double, cols = weights.shape
    tokens = act_t.shape[1]
    part = cols // layers
    whole = lambda a: pl.BlockSpec(a.shape, lambda i, t: (0, 0))
    specs = [
        whole(act_t),
        pl.BlockSpec((1, double, cols), lambda i, t: (t[at + 4 * i + 1], 0, 0)),
        *[whole(e) for e in errs],
    ]
    operands = [act_t, weights, *errs]
    aliases = {}
    if total is not None:
        specs.append(whole(total))
        operands.append(total)
        aliases[len(operands)] = 2
    if held is not None:
        specs.append(pl.BlockSpec(memory_space=pl.ANY))
        operands.append(held)
        aliases[len(operands)] = 0
    body = functools.partial(use_kernel, len(errs), scale, at, total is not None)
    return pl.pallas_call(
        body,
        grid_spec=pltpu.PrefetchScalarGridSpec(
            num_scalar_prefetch=1,
            grid=(m,),
            in_specs=specs,
            out_specs=[
                pl.BlockSpec(
                    (feats, layers, part), lambda i, t: (0, 0, t[at + 4 * i + 3])
                ),
                pl.BlockSpec((1, feats, cols), lambda i, t: (i, 0, 0)),
                pl.BlockSpec((tokens, double), lambda i, t: (0, 0)),
            ],
        ),
        out_shape=[
            jax.ShapeDtypeStruct(shape, BF16),
            jax.ShapeDtypeStruct((m, feats, cols), BF16),
            jax.ShapeDtypeStruct((tokens, double), F32),
        ],
        input_output_aliases=aliases,
        compiler_params=limits(24),
        cost_estimate=cost(
            4 * m * tokens * double * cols, 2 * m * cols * (tokens + 2 * double)
        ),
    )(table, *operands)


def groups_of(units, steps):
    groups = [[(0, 0)]]
    for s in range(1, steps + 1):
        groups.append([(s, -1), (s, 1)] if 2 * s < units else [(s, 0)])
    return groups


def turn_kernel(rows, out):
    out[...] = rows[...].T


def turned(rows):
    return pl.pallas_call(
        turn_kernel,
        out_shape=jax.ShapeDtypeStruct(rows.shape[::-1], rows.dtype),
        compiler_params=limits(12),
        cost_estimate=cost(0, 4 * rows.size),
    )(rows)


def tables(line, ends, units, steps, chains):
    groups = groups_of(units, steps)
    rows = []
    for spot in range(2 * line):
        pos, side = divmod(spot, 2)
        centre = pos + ends - 1

        def taken(s, d):
            if d or not s:
                return d, (centre + d * s) % units, 1
            if centre - s >= 0:
                return -1, centre - s, 1
            if centre + s < units:
                return 1, centre + s, 1
            return 0, centre, 0

        row, at = [], {}

        def add(name, values):
            at[name] = len(row)
            row.extend(values)

        add("prep_a", [(1 - side) * chains])
        add("prep_b", [side * chains])
        add(
            "prep_c",
            [of * chains + k for of in (1 - side, side) for k in range(1, chains)],
        )
        sign = -1 if pos < line // 2 else 1
        add(
            "goals",
            [
                (side * chains + k) * units + centre + sign * e
                for k in range(chains)
                for e in range(ends)
            ],
        )
        for k in range(chains):
            base = (side * chains + k) * units
            for i, group in enumerate(groups):
                values = []
                came = [e for e in group if e[0]]
                for s, d in group:
                    way, unit, valid = taken(s, d)
                    src = 0
                    if way:
                        src = 1 + 2 * sorted({e[0] for e in came}).index(s) + (way > 0)
                    values += [src, unit, valid, base + unit]
                add(f"use_{k}_{i}", values)
        far = [
            [
                [((1 - side) * chains + k) * units + taken(s, d)[1] for s, d in group]
                for group in groups
            ]
            for k in range(chains)
        ]
        for k in range(chains):
            add(f"far_{k}", sum(far[k][:-1], []))
        add("far_last", sum((far[k][-1] for k in range(chains)), []))
        rows.append(row)
    return np.array(rows, np.int32), at


def microstep(resid, enc_weight, enc_bias, dec_weight, dec_bias):
    tokens, _, width = resid.shape
    feats = enc_weight.shape[2]
    scale = 1.0 / math.sqrt(tokens)
    n_cuts = lax.axis_size("cuts")
    bits = n_cuts.bit_length() - 1
    line = lax.axis_size("layer") // 2
    spot = lax.axis_index("layer")
    pos = spot // 2
    cut = lax.axis_index("cuts")
    ups = [(cut >> b) % 2 == 1 for b in range(bits)]
    half = width // 2
    ends = ENDS if half % (128 * (line - 2 + 2 * ENDS)) == 0 else 1
    units = line - 2 + 2 * ends
    steps = line - 2 + ends
    chains = CHAINS
    while chains > 1 and half % (128 * units * chains):
        chains //= 2
    span = half // chains
    part = span // units
    centre = pos + ends - 1
    rows, at = tables(line, ends, units, steps, chains)
    table = lax.dynamic_index_in_dim(jnp.asarray(rows), spot, 0, keepdims=False)

    give = prep(dec_weight, table, at["prep_a"], 1, span, units, 60)
    got = [swap(give[0], "layer", 0)]

    z = dot(resid.reshape(tokens, -1), enc_weight.reshape(-1, feats), ((1,), (0,)))
    held = prep(dec_weight, table, at["prep_b"], 1, span, units)
    own = [held[0]]
    for b in range(bits):
        stay, go = halves(z, ups[b])
        come = swap(go, "cuts", b)
        z = stay + come
    act_mine = jnp.maximum(z + enc_bias[None, :], 0.0).astype(BF16)
    come = swap(act_mine, "layer", 0)
    for k in range(1, chains):
        held = prep(dec_weight, table, at["prep_c"] + k - 1, 1, span, units)
        got.append(swap(held[0], "layer", 0))
        held = prep(dec_weight, table, at["prep_c"] + chains + k - 2, 1, span, units)
        own.append(held[0])
    act = jnp.concatenate([act_mine, come], 1)
    for b in reversed(range(bits)):
        come = swap(act, "cuts", b)
        act = joined(act, come, ups[b])
    goals = goals_of(resid, dec_bias, table, at["goals"], chains * ends, part)

    def shift(value, step, sources):
        pairs = [
            (2 * i + s, 2 * (i + step) + s)
            for i in sources
            if 0 <= i < line and 0 <= i + step < line
            for s in range(2)
        ]
        return lax.ppermute(value, "layer", pairs)

    both = [
        lax.optimization_barrier(jnp.concatenate([own[k], got[k]], 1))
        for k in range(chains)
    ]
    act_t = turned(act)

    def weights(k, u):
        return lax.dynamic_index_in_dim(both[k], u, 0, keepdims=False)

    def recon(k, u):
        return dot(act, weights(k, u), ((1,), (0,)))

    right, left = [None] * chains, [None] * chains
    errs = [[None] * ends for _ in range(chains)]
    for s in range(1, steps + 1):
        for k in range(chains):
            r = recon(k, jnp.clip(units - s + pos, 0, units - 1))
            l = recon(k, jnp.clip(s - line + pos, 0, units - 1))
            if s > 1:
                r = r + right[k].astype(F32)
                l = l + left[k].astype(F32)
            right[k] = shift(r.astype(BF16), 1, range(0, s))
            left[k] = shift(l.astype(BF16), -1, range(line - s, line))
            late = steps - s
            if late < ends:
                u = jnp.where(pos < line // 2, centre - late, centre + late)
                err = recon(k, u) + right[k].astype(F32) + left[k].astype(F32)
                err = err + goals[k * ends + late]
                errs[k][late] = err.astype(BF16)

    dact = dec_grad = None
    fars = [[] for _ in range(chains)]
    groups = groups_of(units, steps)
    right = [errs[k][0] for k in range(chains)]
    left = [errs[k][0] for k in range(chains)]
    came = [[] for _ in range(chains)]

    def put(name, which, dec_grad):
        return place(which, table, at[name], dec_weight.shape, dec_grad)

    for s in range(steps + 1):
        for k in range(chains if s else 0):
            right[k] = shift(right[k], 1, range(max(s - ends, 0), line - 1))
            left[k] = shift(
                left[k], -1, range(1, min(line - 1 + ends - s, line - 1) + 1)
            )
            if s < ends:
                right[k] = jnp.where(pos == 0, errs[k][s], right[k])
                left[k] = jnp.where(pos == line - 1, errs[k][s], left[k])
            came[k] += [right[k], left[k]]
        for k in range(chains):
            for i, group in enumerate(groups):
                if group[-1][0] != s:
                    continue
                if i == len(groups) - 1 and k == chains - 1:
                    for c in range(chains):
                        dec_grad = put(f"far_{c}", fars[c][:i], dec_grad)
                dec_grad, far, dact = use_of(
                    act_t,
                    both[k],
                    [errs[k][0], *came[k]],
                    dact,
                    dec_grad,
                    table,
                    at[f"use_{k}_{i}"],
                    len(group),
                    dec_weight.shape,
                    scale,
                )
                came[k] = []
                fars[k].append(swap(far, "layer", 0))
    dec_grad = put("far_last", [f[-1] for f in fars], dec_grad)

    flats = []
    for i in range(FLATS):
        flats.append(flat_of(resid, i, FLATS, 4))

    for b in range(bits):
        stay, go = halves(dact, ups[b])
        come = swap(go.astype(BF16), "cuts", b).astype(F32)
        dact = stay + come
    come = swap(dact[:, feats:].astype(BF16), "layer", 0).astype(F32)
    dact = dact[:, :feats] + come
    dz = jnp.where(act_mine > 0, dact * scale, 0.0).astype(BF16)
    for b in reversed(range(bits)):
        come = swap(dz, "cuts", b)
        dz = joined(dz, come, ups[b])
    enc_grad = enc_grad_of(flats, dz, 2)
    return enc_grad, dec_grad


def solution(mesh):
    placed = (
        P(None, None, "cuts"),
        P(None, "cuts", "layer"),
        P("layer"),
        P("layer", None, "cuts"),
        P(None, "cuts"),
    )
    return jax.shard_map(
        microstep,
        mesh=mesh,
        in_specs=placed,
        out_specs=(P(None, "cuts", "layer"), P("layer", None, "cuts")),
        check_vma=False,
    )
```

```python
import functools
import math

import jax
import jax.numpy as jnp
import numpy as np
from jax import lax
from jax.experimental import pallas as pl
from jax.experimental.pallas import tpu as pltpu
from jax.sharding import PartitionSpec as P


F32 = jnp.float32
BF16 = jnp.bfloat16
ENDS = 1
CHAINS = 2
FLATS = 4


def swap(value, axis, bit):
    size = lax.axis_size(axis)
    return lax.ppermute(value, axis, [(i, i ^ (1 << bit)) for i in range(size)])


def halves(value, upper):
    half = value.shape[0] // 2
    low, high = value[:half], value[half:]
    return jnp.where(upper, high, low), jnp.where(upper, low, high)


def joined(mine, theirs, upper):
    return jnp.where(
        upper,
        jnp.concatenate([theirs, mine], 0),
        jnp.concatenate([mine, theirs], 0),
    )


def dot(a, b, dims):
    return lax.dot_general(a, b, (dims, ((), ())), preferred_element_type=F32)


def limits(mib):
    return pltpu.CompilerParams(vmem_limit_bytes=mib << 20)


def cost(flops, moved):
    return pl.CostEstimate(flops=flops, bytes_accessed=moved, transcendentals=0)


def enc_grad_kernel(*refs):
    *rows, dz, out = refs
    left = jnp.concatenate([r[0] for r in rows], 0)
    out[0] = dot(left, dz[...], ((0,), (0,))).astype(out.dtype)


def enc_grad_of(rows, dz, blocks):
    layers, size, width = rows[0].shape
    tokens, feats = dz.shape
    block = width // blocks
    return pl.pallas_call(
        enc_grad_kernel,
        grid=(layers, blocks),
        in_specs=[pl.BlockSpec((1, size, block), lambda l, i: (l, 0, i)) for _ in rows]
        + [pl.BlockSpec(dz.shape, lambda l, i: (0, 0))],
        out_specs=pl.BlockSpec((1, block, feats), lambda l, i: (l, i, 0)),
        out_shape=jax.ShapeDtypeStruct((layers, width, feats), BF16),
        compiler_params=limits(24),
        cost_estimate=cost(
            2 * tokens * layers * width * feats, 2 * layers * width * (tokens + feats)
        ),
    )(*rows, dz)


def prep_kernel(table, rows, out):
    _, units, feats, cols = out.shape
    layers = rows.shape[1]
    part = cols // layers
    size = feats * layers
    to = lax.broadcasted_iota(jnp.int32, (size, size), 0)
    at = lax.broadcasted_iota(jnp.int32, (size, size), 1)
    order = jnp.where(at == layers * (to % feats) + to // feats, 1.0, 0.0).astype(BF16)
    flat = rows[...].reshape(size, units * part)
    flat = dot(order, flat, ((1,), (0,))).astype(BF16)
    for u in range(units):
        for layer in range(layers):
            out[0, u, :, layer * part : (layer + 1) * part] = flat[
                layer * feats : (layer + 1) * feats, u * part : (u + 1) * part
            ]


def prep(weight, table, at, count, span, units, room=16):
    feats, layers, _ = weight.shape
    cols = layers * span // units
    return pl.pallas_call(
        prep_kernel,
        grid_spec=pltpu.PrefetchScalarGridSpec(
            num_scalar_prefetch=1,
            grid=(count,),
            in_specs=[
                pl.BlockSpec((feats, layers, span), lambda i, t: (0, 0, t[at + i]))
            ],
            out_specs=pl.BlockSpec((1, units, feats, cols), lambda i, t: (i, 0, 0, 0)),
        ),
        out_shape=jax.ShapeDtypeStruct((count, units, feats, cols), BF16),
        compiler_params=limits(room),
        cost_estimate=cost(0, 4 * count * feats * layers * span),
    )(table, weight)


def place_kernel(count, at, sizes, table, *refs):
    groups, out, sems = refs[:count], refs[-2], refs[-1]
    part = groups[0].shape[3]
    copies = []
    for j, size in enumerate(sizes):
        for i in range(size):
            entry = at + 2 * len(copies)
            start = pl.multiple_of(table[entry] * part, part)
            copy = pltpu.make_async_copy(
                groups[j].at[i], out.at[:, :, pl.ds(start, part)], sems.at[len(copies)]
            )
            copies.append((copy, table[entry + 1] == 1))
    for copy, valid in copies:

        @pl.when(valid)
        def _(copy=copy):
            copy.start()

    for copy, valid in copies:

        @pl.when(valid)
        def _(copy=copy):
            copy.wait()


def place(groups, table, at, held):
    sizes = [g.shape[0] for g in groups]
    body = functools.partial(place_kernel, len(groups), at, sizes)
    return pl.pallas_call(
        body,
        grid_spec=pltpu.PrefetchScalarGridSpec(
            num_scalar_prefetch=1,
            grid=(1,),
            in_specs=[pl.BlockSpec(g.shape, lambda i, t: (0, 0, 0, 0)) for g in groups]
            + [pl.BlockSpec(memory_space=pl.ANY)],
            out_specs=pl.BlockSpec(memory_space=pl.ANY),
            scratch_shapes=[pltpu.SemaphoreType.DMA((sum(sizes),))],
        ),
        out_shape=jax.ShapeDtypeStruct(held.shape, held.dtype),
        input_output_aliases={len(groups) + 1: 0},
        compiler_params=limits(16),
        cost_estimate=cost(0, 4 * sum(g.size for g in groups)),
    )(table, *groups, held)


def goal_kernel(ends, units, at, table, resid, bias, out):
    layers = resid.shape[1]
    part = resid.shape[2] // units
    for e in range(ends):
        entry = at + 1 + e
        here = pl.ds(pl.multiple_of(table[entry] * part, part), part)
        for layer in range(layers):
            rows = resid[:, layer, here].astype(F32)
            out[0, e, :, layer * part : (layer + 1) * part] = (
                bias[layer, here][None, :] - rows
            )


def goals_of(resid, bias, table, at, chains, ends, units, part):
    tokens, layers, _ = resid.shape
    wide = units // 2 * part

    def block(i, t):
        return t[at] + 2 * i

    return pl.pallas_call(
        functools.partial(goal_kernel, ends, units // 2, at),
        grid_spec=pltpu.PrefetchScalarGridSpec(
            num_scalar_prefetch=1,
            grid=(chains,),
            in_specs=[
                pl.BlockSpec((tokens, layers, wide), lambda i, t: (0, 0, block(i, t))),
                pl.BlockSpec((layers, wide), lambda i, t: (0, block(i, t))),
            ],
            out_specs=pl.BlockSpec(
                (1, ends, tokens, layers * part), lambda i, t: (i, 0, 0, 0)
            ),
        ),
        out_shape=jax.ShapeDtypeStruct((chains, ends, tokens, layers * part), F32),
        compiler_params=limits(24),
        cost_estimate=cost(0, 6 * chains * ends * tokens * layers * part),
    )(table, resid, bias)


def flat_kernel(rows, out):
    layers, count, block = out.shape
    size = count * layers
    to = lax.broadcasted_iota(jnp.int32, (size, size), 0)
    at = lax.broadcasted_iota(jnp.int32, (size, size), 1)
    order = jnp.where(at == layers * (to % count) + to // count, 1.0, 0.0).astype(BF16)
    flat = dot(order, rows[...].reshape(size, block), ((1,), (0,))).astype(BF16)
    for layer in range(layers):
        out[layer] = flat[layer * count : (layer + 1) * count]


def flat_of(resid, piece, pieces, blocks):
    tokens, layers, width = resid.shape
    size, block = tokens // pieces, width // blocks
    return pl.pallas_call(
        flat_kernel,
        grid=(blocks,),
        in_specs=[pl.BlockSpec((size, layers, block), lambda i: (piece, 0, i))],
        out_specs=pl.BlockSpec((layers, size, block), lambda i: (0, 0, i)),
        out_shape=jax.ShapeDtypeStruct((layers, size, width), BF16),
        compiler_params=limits(12),
        cost_estimate=cost(0, 4 * size * layers * width),
    )(resid)


def use_kernel(n, scale, at, has_sum, table, act_t, weights, *refs):
    errs, rest = refs[:n], refs[n:]
    near, far, total = rest[-3:]
    step = pl.program_id(0)
    base = at + 4 * step
    src, valid = table[base], table[base + 2]
    if n == 1:
        e = errs[0][...]
    else:
        e = jnp.where(src == 0, errs[0][...], errs[1][...])
        for j in range(2, n):
            e = jnp.where(src == j, errs[j][...], e)
    feats, layers, part = near.shape
    grad = (dot(act_t[...], e, ((1,), (0,))) * scale).astype(BF16)
    for layer in range(layers):
        columns = slice(layer * part, (layer + 1) * part)
        near[:, layer, :] = grad[:feats, columns]
        far[0, :, layer, :] = grad[feats:, columns]
    more = dot(e, weights[0], ((1,), (1,))) * valid.astype(F32)

    @pl.when(step == 0)
    def _():
        total[...] = rest[0][...] + more if has_sum else more

    @pl.when(step > 0)
    def _():
        total[...] += more


def use_of(act_t, weights, errs, total, held, table, at, m, shape, scale):
    feats, layers, _ = shape
    _, double, cols = weights.shape
    tokens = act_t.shape[1]
    part = cols // layers
    whole = lambda a: pl.BlockSpec(a.shape, lambda i, t: (0, 0))
    specs = [
        whole(act_t),
        pl.BlockSpec((1, double, cols), lambda i, t: (t[at + 4 * i + 1], 0, 0)),
        *[whole(e) for e in errs],
    ]
    operands = [act_t, weights, *errs]
    aliases = {}
    if total is not None:
        specs.append(whole(total))
        operands.append(total)
        aliases[len(operands)] = 2
    if held is not None:
        specs.append(pl.BlockSpec(memory_space=pl.ANY))
        operands.append(held)
        aliases[len(operands)] = 0
    body = functools.partial(use_kernel, len(errs), scale, at, total is not None)
    return pl.pallas_call(
        body,
        grid_spec=pltpu.PrefetchScalarGridSpec(
            num_scalar_prefetch=1,
            grid=(m,),
            in_specs=specs,
            out_specs=[
                pl.BlockSpec(
                    (feats, layers, part), lambda i, t: (0, 0, t[at + 4 * i + 3])
                ),
                pl.BlockSpec((1, feats, layers, part), lambda i, t: (i, 0, 0, 0)),
                pl.BlockSpec((tokens, double), lambda i, t: (0, 0)),
            ],
        ),
        out_shape=[
            jax.ShapeDtypeStruct(shape, BF16),
            jax.ShapeDtypeStruct((m, feats, layers, part), BF16),
            jax.ShapeDtypeStruct((tokens, double), F32),
        ],
        input_output_aliases=aliases,
        compiler_params=limits(24),
        cost_estimate=cost(
            4 * m * tokens * double * cols, 2 * m * cols * (tokens + 2 * double)
        ),
    )(table, *operands)


def groups_of(units, steps):
    several = 1 if units == steps + 1 else 2
    groups, now = [[(0, 0)]], []
    for s in range(1, steps + 1):
        now += [(s, -1), (s, 1)] if 2 * s < units else [(s, 0)]
        if s % several == 0 or s == steps:
            groups.append(now)
            now = []
    return groups


def turn_kernel(rows, out):
    out[...] = rows[...].T


def turned(rows):
    return pl.pallas_call(
        turn_kernel,
        out_shape=jax.ShapeDtypeStruct(rows.shape[::-1], rows.dtype),
        compiler_params=limits(12),
        cost_estimate=cost(0, 4 * rows.size),
    )(rows)


def tables(line, ends, units, steps, chains):
    groups = groups_of(units, steps)
    rows = []
    for spot in range(2 * line):
        pos, side = divmod(spot, 2)
        centre = pos + ends - 1

        def taken(s, d):
            if d or not s:
                return d, (centre + d * s) % units, 1
            if centre - s >= 0:
                return -1, centre - s, 1
            if centre + s < units:
                return 1, centre + s, 1
            return 0, centre, 0

        row, at = [], {}

        def add(name, values):
            at[name] = len(row)
            row.extend(values)

        add("prep_a", [(1 - side) * chains])
        add("prep_b", [side * chains])
        add(
            "prep_c",
            [of * chains + k for of in (1 - side, side) for k in range(1, chains)],
        )
        sign = -1 if pos < line // 2 else 1
        block = int(pos >= line // 2)
        add("goals", [2 * side * chains + block])
        add("goals_at", [(centre + sign * e) % (units // 2) for e in range(ends)])
        add("edges", [int(pos in (0, line - 1))] * chains * ends)
        for k in range(chains):
            base = (side * chains + k) * units
            for i, group in enumerate(groups):
                values = []
                came = [e for e in group if e[0]]
                for s, d in group:
                    way, unit, valid = taken(s, d)
                    src = 0
                    if way:
                        src = 1 + 2 * sorted({e[0] for e in came}).index(s)
                        src += int((way < 0) == (pos % 2 == 0))
                    values += [src, unit, valid, base + unit]
                add(f"use_{k}_{i}", values)
        for k in range(chains):
            base = ((1 - side) * chains + k) * units
            values = []
            for s, d in sum(groups, []):
                _, unit, valid = taken(s, d)
                if d and not 0 <= centre + d * s < units:
                    valid = 0
                values += [base + unit, valid]
            add(f"far_{k}", values)
        rows.append(row)
    return np.array(rows, np.int32), at


def microstep(resid, enc_weight, enc_bias, dec_weight, dec_bias):
    tokens, _, width = resid.shape
    feats = enc_weight.shape[2]
    scale = 1.0 / math.sqrt(tokens)
    n_cuts = lax.axis_size("cuts")
    bits = n_cuts.bit_length() - 1
    line = lax.axis_size("layer") // 2
    spot = lax.axis_index("layer")
    pos = spot // 2
    cut = lax.axis_index("cuts")
    ups = [(cut >> b) % 2 == 1 for b in range(bits)]
    half = width // 2
    ends = ENDS if half % (128 * (line - 2 + 2 * ENDS)) == 0 else 1
    units = line - 2 + 2 * ends
    steps = line - 2 + ends
    chains = CHAINS
    while chains > 1 and half % (128 * units * chains):
        chains //= 2
    span = half // chains
    part = span // units
    centre = pos + ends - 1
    rows, at = tables(line, ends, units, steps, chains)
    table = lax.dynamic_index_in_dim(jnp.asarray(rows), spot, 0, keepdims=False)

    give = prep(dec_weight, table, at["prep_a"], 1, span, units, 60)
    got = [swap(give[0], "layer", 0)]

    z = dot(resid.reshape(tokens, -1), enc_weight.reshape(-1, feats), ((1,), (0,)))
    held = prep(dec_weight, table, at["prep_b"], 1, span, units)
    own = [held[0]]
    for b in range(bits):
        stay, go = halves(z, ups[b])
        come = swap(go, "cuts", b)
        z = stay + come
    act_mine = jnp.maximum(z + enc_bias[None, :], 0.0).astype(BF16)
    come = swap(act_mine, "layer", 0)
    for k in range(1, chains):
        held = prep(dec_weight, table, at["prep_c"] + k - 1, 1, span, units)
        got.append(swap(held[0], "layer", 0))
        held = prep(dec_weight, table, at["prep_c"] + chains + k - 2, 1, span, units)
        own.append(held[0])
    act = jnp.concatenate([act_mine, come], 1)
    for b in reversed(range(bits)):
        come = swap(act, "cuts", b)
        act = joined(act, come, ups[b])
    goals = goals_of(
        resid, dec_bias, table, at["goals"], chains, ends, units, part
    )

    def exchange(value, ups, downs, even):
        pairs = [
            (2 * i + s, 2 * j + s)
            for i in range(line)
            for j, sources in ((i + 1, ups), (i - 1, downs))
            if i in sources and 0 <= j < line and (i % 2 == 0) == (even == (j > i))
            for s in range(2)
        ]
        if not pairs:
            return None
        return lax.ppermute(value, "layer", pairs)

    def plus(value, more):
        return value if more is None else value + more.astype(F32)

    even = pos % 2 == 0

    both = [
        lax.optimization_barrier(jnp.concatenate([own[k], got[k]], 1))
        for k in range(chains)
    ]
    act_t = turned(act)

    def weights(k, u):
        return lax.dynamic_index_in_dim(both[k], u, 0, keepdims=False)

    def recon(k, u):
        return dot(act, weights(k, u), ((1,), (0,)))

    ahead, behind = [None] * chains, [None] * chains
    errs = [[None] * ends for _ in range(chains)]
    for s in range(1, steps + 1):
        up, down = units - s + pos, s - line + pos
        one = jnp.clip(jnp.where(even, up, down), 0, units - 1)
        two = jnp.clip(jnp.where(even, down, up), 0, units - 1)
        ways = range(0, s), range(line - s, line)
        for k in range(chains):
            give = plus(recon(k, one), behind[k]).astype(BF16)
            first = exchange(give, *ways, True)
            behind_next = None
            if s > 1:
                give = plus(recon(k, two), ahead[k]).astype(BF16)
                behind_next = exchange(give, *ways, False)
            ahead[k], behind[k] = first, behind_next
            late = steps - s
            if late < ends:
                u = jnp.where(pos < line // 2, centre - late, centre + late)
                err = plus(plus(recon(k, u), ahead[k]), behind[k])
                err = err + goals[k, late]
                errs[k][late] = err.astype(BF16)

    dact = dec_grad = None
    fars = [[] for _ in range(chains)]
    groups = groups_of(units, steps)
    ahead = [errs[k][0] for k in range(chains)]
    behind = [errs[k][0] for k in range(chains)]
    came = [[] for _ in range(chains)]

    def put(name, which, dec_grad):
        return place(which, table, at[name], dec_grad)

    for s in range(steps + 1):
        ways = range(max(s - ends, 0), line - 1), range(1, line + min(ends - s, 0))
        for k in range(chains if s else 0):
            first = exchange(behind[k], *ways, True)
            second = exchange(ahead[k], *ways, False)
            if 0 < s < ends:
                edge = table[at["edges"] + k * ends + s].astype(BF16)
                second = second + errs[k][s] * edge
            ahead[k], behind[k] = first, second
            came[k] += [first, first if second is None else second]
        for k in range(chains):
            for i, group in enumerate(groups):
                if group[-1][0] != s:
                    continue
                dec_grad, far, dact = use_of(
                    act_t,
                    both[k],
                    [errs[k][0], *came[k]],
                    dact,
                    dec_grad,
                    table,
                    at[f"use_{k}_{i}"],
                    len(group),
                    dec_weight.shape,
                    scale,
                )
                came[k] = []
                fars[k].append(swap(far, "layer", 0))
    for k in range(chains):
        dec_grad = put(f"far_{k}", fars[k], dec_grad)

    flats = []
    for i in range(FLATS):
        flats.append(flat_of(resid, i, FLATS, 4))

    for b in range(bits):
        stay, go = halves(dact, ups[b])
        come = swap(go.astype(BF16), "cuts", b).astype(F32)
        dact = stay + come
    come = swap(dact[:, feats:].astype(BF16), "layer", 0).astype(F32)
    dact = dact[:, :feats] + come
    dz = jnp.where(act_mine > 0, dact * scale, 0.0).astype(BF16)
    for b in reversed(range(bits)):
        come = swap(dz, "cuts", b)
        dz = joined(dz, come, ups[b])
    enc_grad = enc_grad_of(flats, dz, 2)
    return enc_grad, dec_grad


def solution(mesh):
    placed = (
        P(None, None, "cuts"),
        P(None, "cuts", "layer"),
        P("layer"),
        P("layer", None, "cuts"),
        P(None, "cuts"),
    )
    return jax.shard_map(
        microstep,
        mesh=mesh,
        in_specs=placed,
        out_specs=(P(None, "cuts", "layer"), P("layer", None, "cuts")),
        check_vma=False,
    )
```

```python
import functools
import math

import jax
import jax.numpy as jnp
import numpy as np
from jax import lax
from jax.experimental import pallas as pl
from jax.experimental.pallas import tpu as pltpu
from jax.sharding import PartitionSpec as P


F32 = jnp.float32
BF16 = jnp.bfloat16
ENDS = 3
CHAINS = 2
FLATS = 4


def swap(value, axis, bit):
    size = lax.axis_size(axis)
    return lax.ppermute(value, axis, [(i, i ^ (1 << bit)) for i in range(size)])


def halves(value, upper):
    half = value.shape[0] // 2
    low, high = value[:half], value[half:]
    return jnp.where(upper, high, low), jnp.where(upper, low, high)


def joined(mine, theirs, upper):
    return jnp.where(
        upper,
        jnp.concatenate([theirs, mine], 0),
        jnp.concatenate([mine, theirs], 0),
    )


def dot(a, b, dims):
    return lax.dot_general(a, b, (dims, ((), ())), preferred_element_type=F32)


def limits(mib):
    return pltpu.CompilerParams(vmem_limit_bytes=mib << 20)


def cost(flops, moved):
    return pl.CostEstimate(flops=flops, bytes_accessed=moved, transcendentals=0)


def enc_grad_kernel(*refs):
    *rows, dz, out = refs
    left = jnp.concatenate([r[0] for r in rows], 0)
    out[0] = dot(left, dz[...], ((0,), (0,))).astype(out.dtype)


def enc_grad_of(rows, dz, blocks):
    layers, size, width = rows[0].shape
    tokens, feats = dz.shape
    block = width // blocks
    return pl.pallas_call(
        enc_grad_kernel,
        grid=(layers, blocks),
        in_specs=[pl.BlockSpec((1, size, block), lambda l, i: (l, 0, i)) for _ in rows]
        + [pl.BlockSpec(dz.shape, lambda l, i: (0, 0))],
        out_specs=pl.BlockSpec((1, block, feats), lambda l, i: (l, i, 0)),
        out_shape=jax.ShapeDtypeStruct((layers, width, feats), BF16),
        compiler_params=limits(24),
        cost_estimate=cost(
            2 * tokens * layers * width * feats, 2 * layers * width * (tokens + feats)
        ),
    )(*rows, dz)


def prep_kernel(table, rows, out):
    _, units, feats, cols = out.shape
    layers = rows.shape[1]
    part = cols // layers
    size = feats * layers
    to = lax.broadcasted_iota(jnp.int32, (size, size), 0)
    at = lax.broadcasted_iota(jnp.int32, (size, size), 1)
    order = jnp.where(at == layers * (to % feats) + to // feats, 1.0, 0.0).astype(BF16)
    flat = rows[...].reshape(size, units * part)
    flat = dot(order, flat, ((1,), (0,))).astype(BF16)
    for u in range(units):
        for layer in range(layers):
            out[0, u, :, layer * part : (layer + 1) * part] = flat[
                layer * feats : (layer + 1) * feats, u * part : (u + 1) * part
            ]


def prep(weight, table, at, count, span, units, room=16):
    feats, layers, _ = weight.shape
    cols = layers * span // units
    return pl.pallas_call(
        prep_kernel,
        grid_spec=pltpu.PrefetchScalarGridSpec(
            num_scalar_prefetch=1,
            grid=(count,),
            in_specs=[
                pl.BlockSpec((feats, layers, span), lambda i, t: (0, 0, t[at + i]))
            ],
            out_specs=pl.BlockSpec((1, units, feats, cols), lambda i, t: (i, 0, 0, 0)),
        ),
        out_shape=jax.ShapeDtypeStruct((count, units, feats, cols), BF16),
        compiler_params=limits(room),
        cost_estimate=cost(0, 4 * count * feats * layers * span),
    )(table, weight)


def place_kernel(count, at, sizes, table, *refs):
    groups, out, sems = refs[:count], refs[-2], refs[-1]
    part = groups[0].shape[3]
    copies = []
    for j, size in enumerate(sizes):
        for i in range(size):
            entry = at + 2 * len(copies)
            start = pl.multiple_of(table[entry] * part, part)
            copy = pltpu.make_async_copy(
                groups[j].at[i], out.at[:, :, pl.ds(start, part)], sems.at[len(copies)]
            )
            copies.append((copy, table[entry + 1] == 1))
    for copy, valid in copies:

        @pl.when(valid)
        def _(copy=copy):
            copy.start()

    for copy, valid in copies:

        @pl.when(valid)
        def _(copy=copy):
            copy.wait()


def place(groups, table, at, shape, held):
    sizes = [g.shape[0] for g in groups]
    body = functools.partial(place_kernel, len(groups), at, sizes)
    operands = list(groups)
    specs = [pl.BlockSpec(memory_space=pltpu.VMEM)] * len(groups)
    aliases = {}
    if held is not None:
        operands.append(held)
        specs.append(pl.BlockSpec(memory_space=pl.ANY))
        aliases = {len(operands): 0}
    return pl.pallas_call(
        body,
        in_specs=[pl.BlockSpec(memory_space=pltpu.SMEM)] + specs,
        out_specs=pl.BlockSpec(memory_space=pl.ANY),
        scratch_shapes=[pltpu.SemaphoreType.DMA((sum(sizes),))],
        out_shape=jax.ShapeDtypeStruct(shape, BF16),
        input_output_aliases=aliases,
        compiler_params=limits(16),
        cost_estimate=cost(0, 4 * sum(g.size for g in groups)),
    )(table, *operands)


def goal_kernel(ends, units, at, table, resid, bias, out):
    layers = resid.shape[1]
    part = resid.shape[2] // units
    for e in range(ends):
        entry = at + 1 + e
        here = pl.ds(pl.multiple_of(table[entry] * part, part), part)
        for layer in range(layers):
            rows = resid[:, layer, here].astype(F32)
            out[0, e, :, layer * part : (layer + 1) * part] = (
                bias[layer, here][None, :] - rows
            )


def goals_of(resid, bias, table, at, chains, ends, units, part):
    tokens, layers, _ = resid.shape
    wide = units // 2 * part
    rows = tokens // 4

    def block(i, t):
        return t[at] + 2 * i

    return pl.pallas_call(
        functools.partial(goal_kernel, ends, units // 2, at),
        grid_spec=pltpu.PrefetchScalarGridSpec(
            num_scalar_prefetch=1,
            grid=(chains, 4),
            in_specs=[
                pl.BlockSpec((rows, layers, wide), lambda i, j, t: (j, 0, block(i, t))),
                pl.BlockSpec((layers, wide), lambda i, j, t: (0, block(i, t))),
            ],
            out_specs=pl.BlockSpec(
                (1, ends, rows, layers * part), lambda i, j, t: (i, 0, j, 0)
            ),
        ),
        out_shape=jax.ShapeDtypeStruct((chains, ends, tokens, layers * part), F32),
        compiler_params=limits(12),
        cost_estimate=cost(0, 6 * chains * ends * tokens * layers * part),
    )(table, resid, bias)


def flat_kernel(rows, out):
    layers, count, block = out.shape
    size = count * layers
    to = lax.broadcasted_iota(jnp.int32, (size, size), 0)
    at = lax.broadcasted_iota(jnp.int32, (size, size), 1)
    order = jnp.where(at == layers * (to % count) + to // count, 1.0, 0.0).astype(BF16)
    flat = dot(order, rows[...].reshape(size, block), ((1,), (0,))).astype(BF16)
    for layer in range(layers):
        out[layer] = flat[layer * count : (layer + 1) * count]


def flat_of(resid, piece, pieces, blocks):
    tokens, layers, width = resid.shape
    size, block = tokens // pieces, width // blocks
    return pl.pallas_call(
        flat_kernel,
        grid=(blocks,),
        in_specs=[pl.BlockSpec((size, layers, block), lambda i: (piece, 0, i))],
        out_specs=pl.BlockSpec((layers, size, block), lambda i: (0, 0, i)),
        out_shape=jax.ShapeDtypeStruct((layers, size, width), BF16),
        compiler_params=limits(12),
        cost_estimate=cost(0, 4 * size * layers * width),
    )(resid)


def use_kernel(kinds, n, scale, at, has_sum, table, act_t, *refs):
    m = len(kinds)
    weights, errs, rest = refs[0], refs[1 : n + 1], refs[n + 1 :]
    near, far, total, given = rest[-4:]
    feats, layers, part = near.shape[1:]
    cols = layers * part
    found, added = [], []
    for i, kind in enumerate(kinds):
        entry = at + 3 * i
        e = errs[kind[0]][...]
        for j in kind[1:]:
            e = jnp.where(table[entry] == j, errs[j][...], e)
        found.append(e)
        added.append(e * table[entry + 2].astype(BF16) if 0 in kind[1:] else e)

    def grads(i, e):
        grad = (dot(act_t[...], e, ((1,), (0,))) * scale).astype(BF16)
        for layer in range(layers):
            columns = slice(layer * part, (layer + 1) * part)
            near[i, :, layer, :] = grad[:feats, columns]
            far[i, :, layer, :] = grad[feats:, columns]

    if m == 1:
        grads(0, found[0])
    else:
        given[...] = jnp.concatenate(found, 1)

        def one(i, _):
            grads(i, given[:, pl.ds(pl.multiple_of(i * cols, cols), cols)])
            return 0

        lax.fori_loop(0, m, one, 0)
    e = jnp.concatenate(added, 1)
    w = jnp.concatenate([weights[table[at + 3 * i + 1]] for i in range(m)], 1)
    more = dot(e, w, ((1,), (1,)))
    total[...] = rest[0][...] + more if has_sum else more


def use_of(act_t, weights, errs, total, table, at, kinds, shape, scale):
    feats, layers, _ = shape
    _, double, cols = weights.shape
    tokens = act_t.shape[1]
    m, n = len(kinds), len(errs)
    part = cols // layers

    outs = [
        jax.ShapeDtypeStruct((m, feats, layers, part), BF16),
        jax.ShapeDtypeStruct((m, feats, layers, part), BF16),
        jax.ShapeDtypeStruct((tokens, double), F32),
    ]
    operands = [act_t, weights, *errs]
    if total is not None:
        operands.append(total)
    near_by = pl.BlockSpec(memory_space=pltpu.VMEM)
    return pl.pallas_call(
        functools.partial(use_kernel, kinds, n, scale, at, total is not None),
        in_specs=[pl.BlockSpec(memory_space=pltpu.SMEM)] + [near_by] * len(operands),
        out_specs=[near_by] * 3,
        out_shape=outs,
        scratch_shapes=[pltpu.VMEM((tokens, m * cols), BF16)],
        compiler_params=limits(28),
        cost_estimate=cost(
            4 * m * tokens * double * cols, 2 * m * cols * (tokens + 2 * double)
        ),
    )(table, *operands)


def groups_of(units, steps):
    several = 1 if units == steps + 1 else 2
    groups, now = [[(0, 0)]], []
    for s in range(1, steps + 1):
        now += [(s, -1), (s, 1)] if 2 * s < units else [(s, 0)]
        if s % several == 0 or s == steps:
            groups.append(now)
            now = []
    return groups


def turn_kernel(rows, out):
    out[...] = rows[...].T


def turned(rows):
    return pl.pallas_call(
        turn_kernel,
        out_shape=jax.ShapeDtypeStruct(rows.shape[::-1], rows.dtype),
        compiler_params=limits(12),
        cost_estimate=cost(0, 4 * rows.size),
    )(rows)


def tables(line, ends, units, steps, chains):
    groups = groups_of(units, steps)
    rows = []
    for spot in range(2 * line):
        pos, side = divmod(spot, 2)
        centre = pos + ends - 1

        def taken(s, d):
            if d or not s:
                return d, (centre + d * s) % units, 1
            if centre - s >= 0:
                return -1, centre - s, 1
            if centre + s < units:
                return 1, centre + s, 1
            return 0, centre, 0

        row, at = [], {}

        def add(name, values):
            at[name] = len(row)
            row.extend(values)

        add("prep_a", [(1 - side) * chains])
        add("prep_b", [side * chains])
        add(
            "prep_c",
            [of * chains + k for of in (1 - side, side) for k in range(1, chains)],
        )
        sign = -1 if pos < line // 2 else 1
        block = int(pos >= line // 2)
        add("goals", [2 * side * chains + block])
        add("goals_at", [(centre + sign * e) % (units // 2) for e in range(ends)])
        add("edges", [int(pos in (0, line - 1))] * chains * ends)
        for k in range(chains):
            for i, group in enumerate(groups):
                values = []
                came = sorted({s for s, _ in group if s})
                for s, d in group:
                    way, unit, valid = taken(s, d)
                    src = 0
                    if way:
                        src = 1 + 2 * came.index(s)
                        src += int((way < 0) == (pos % 2 == 0))
                    values += [src, unit, valid]
                add(f"use_{k}_{i}", values)
            values = []
            for group in groups:
                for of in (side, 1 - side):
                    for s, d in group:
                        _, unit, valid = taken(s, d)
                        if d and not 0 <= centre + d * s < units:
                            valid = 0
                        values += [(of * chains + k) * units + unit, valid]
            add(f"place_{k}", values)
        rows.append(row)
    return np.array(rows, np.int32), at


def microstep(resid, enc_weight, enc_bias, dec_weight, dec_bias):
    tokens, _, width = resid.shape
    feats = enc_weight.shape[2]
    scale = 1.0 / math.sqrt(tokens)
    n_cuts = lax.axis_size("cuts")
    bits = n_cuts.bit_length() - 1
    line = lax.axis_size("layer") // 2
    spot = lax.axis_index("layer")
    pos = spot // 2
    cut = lax.axis_index("cuts")
    ups = [(cut >> b) % 2 == 1 for b in range(bits)]
    half = width // 2
    ends = ENDS if half % (128 * (line - 2 + 2 * ENDS)) == 0 else 1
    units = line - 2 + 2 * ends
    steps = line - 2 + ends
    chains = CHAINS
    while chains > 1 and half % (128 * units * chains):
        chains //= 2
    span = half // chains
    part = span // units
    centre = pos + ends - 1
    rows, at = tables(line, ends, units, steps, chains)
    table = lax.dynamic_index_in_dim(jnp.asarray(rows), spot, 0, keepdims=False)

    give = prep(dec_weight, table, at["prep_a"], 1, span, units, 60)
    got = [swap(give[0], "layer", 0)]

    z = dot(resid.reshape(tokens, -1), enc_weight.reshape(-1, feats), ((1,), (0,)))
    held = prep(dec_weight, table, at["prep_b"], 1, span, units)
    own = [held[0]]
    for b in range(bits):
        stay, go = halves(z, ups[b])
        come = swap(go, "cuts", b)
        z = stay + come
    act_mine = jnp.maximum(z + enc_bias[None, :], 0.0).astype(BF16)
    come = swap(act_mine, "layer", 0)
    for k in range(1, chains):
        held = prep(dec_weight, table, at["prep_c"] + k - 1, 1, span, units)
        got.append(swap(held[0], "layer", 0))
        held = prep(dec_weight, table, at["prep_c"] + chains + k - 2, 1, span, units)
        own.append(held[0])
    act = jnp.concatenate([act_mine, come], 1)
    for b in reversed(range(bits)):
        come = swap(act, "cuts", b)
        act = joined(act, come, ups[b])
    goals = goals_of(
        resid, dec_bias, table, at["goals"], chains, ends, units, part
    )

    def exchange(value, ups, downs, even):
        pairs = [
            (2 * i + s, 2 * j + s)
            for i in range(line)
            for j, sources in ((i + 1, ups), (i - 1, downs))
            if i in sources and 0 <= j < line and (i % 2 == 0) == (even == (j > i))
            for s in range(2)
        ]
        if not pairs:
            return None
        return lax.ppermute(value, "layer", pairs)

    def plus(value, more):
        return value if more is None else value + more.astype(F32)

    even = pos % 2 == 0

    both = [
        lax.optimization_barrier(jnp.concatenate([own[k], got[k]], 1))
        for k in range(chains)
    ]
    act_t = turned(act)

    def weights(k, u):
        return lax.dynamic_index_in_dim(both[k], u, 0, keepdims=False)

    def recon(k, u):
        return dot(act, weights(k, u), ((1,), (0,)))

    ahead, behind = [None] * chains, [None] * chains
    errs = [[None] * ends for _ in range(chains)]
    for s in range(1, steps + 1):
        up, down = units - s + pos, s - line + pos
        one = jnp.clip(jnp.where(even, up, down), 0, units - 1)
        two = jnp.clip(jnp.where(even, down, up), 0, units - 1)
        ways = range(0, s), range(line - s, line)
        for k in range(chains):
            give = plus(recon(k, one), behind[k]).astype(BF16)
            first = exchange(give, *ways, True)
            behind_next = None
            if s > 1:
                give = plus(recon(k, two), ahead[k]).astype(BF16)
                behind_next = exchange(give, *ways, False)
            ahead[k], behind[k] = first, behind_next
            late = steps - s
            if late < ends:
                u = jnp.where(pos < line // 2, centre - late, centre + late)
                err = plus(plus(recon(k, u), ahead[k]), behind[k])
                err = err + goals[k, late]
                errs[k][late] = err.astype(BF16)

    dact = dec_grad = None
    grads = [[] for _ in range(chains)]
    groups = groups_of(units, steps)
    ahead = [errs[k][0] for k in range(chains)]
    behind = [errs[k][0] for k in range(chains)]
    came = [[] for _ in range(chains)]

    for s in range(steps + 1):
        ways = range(max(s - ends, 0), line - 1), range(1, line + min(ends - s, 0))
        for k in range(chains if s else 0):
            first = exchange(behind[k], *ways, True)
            second = exchange(ahead[k], *ways, False)
            if 0 < s < ends:
                edge = table[at["edges"] + k * ends + s].astype(BF16)
                second = second + errs[k][s] * edge
            ahead[k], behind[k] = first, second
            came[k] += [first, first if second is None else second]
        for k in range(chains):
            for i, group in enumerate(groups):
                if group[-1][0] != s:
                    continue
                first = sorted({t for t, _ in group if t})
                kinds = [
                    (0,)
                    if not t
                    else tuple(1 + 2 * first.index(t) + j for j in range(2))
                    + (() if d else (0,))
                    for t, d in group
                ]
                near, far, dact = use_of(
                    act_t,
                    both[k],
                    [errs[k][0], *came[k]],
                    dact,
                    table,
                    at[f"use_{k}_{i}"],
                    kinds,
                    dec_weight.shape,
                    scale,
                )
                came[k] = []
                grads[k] += [near, swap(far, "layer", 0)]
    for k in range(chains):
        dec_grad = place(grads[k], table, at[f"place_{k}"], dec_weight.shape, dec_grad)

    flats = []
    for i in range(FLATS):
        flats.append(flat_of(resid, i, FLATS, 4))

    stay, go = halves(dact, ups[0])
    come = swap(go.astype(BF16), "cuts", 0).astype(F32)
    dact = stay + come
    come = swap(dact[:, feats:].astype(BF16), "layer", 0).astype(F32)
    dact = dact[:, :feats] + come
    for b in range(1, bits):
        dact = dact + swap(dact.astype(BF16), "cuts", b).astype(F32)
    live, _ = halves(act[:, :feats], ups[0])
    dz = jnp.where(live > 0, dact * scale, 0.0).astype(BF16)
    come = swap(dz, "cuts", 0)
    dz = joined(dz, come, ups[0])
    enc_grad = enc_grad_of(flats, dz, 2)
    return enc_grad, dec_grad


def solution(mesh):
    placed = (
        P(None, None, "cuts"),
        P(None, "cuts", "layer"),
        P("layer"),
        P("layer", None, "cuts"),
        P(None, "cuts"),
    )
    return jax.shard_map(
        microstep,
        mesh=mesh,
        in_specs=placed,
        out_specs=(P(None, "cuts", "layer"), P("layer", None, "cuts")),
        check_vma=False,
    )
```

```python
import functools
import math

import jax
import jax.numpy as jnp
import numpy as np
from jax import lax
from jax.experimental import pallas as pl
from jax.experimental.pallas import tpu as pltpu
from jax.sharding import PartitionSpec as P


F32 = jnp.float32
BF16 = jnp.bfloat16
ENDS = 3
CHAINS = 2
FLATS = 4


def swap(value, axis, bit):
    size = lax.axis_size(axis)
    return lax.ppermute(value, axis, [(i, i ^ (1 << bit)) for i in range(size)])


def halves(value, upper):
    half = value.shape[0] // 2
    low, high = value[:half], value[half:]
    return jnp.where(upper, high, low), jnp.where(upper, low, high)


def joined(mine, theirs, upper):
    return jnp.where(
        upper,
        jnp.concatenate([theirs, mine], 0),
        jnp.concatenate([mine, theirs], 0),
    )


def dot(a, b, dims):
    return lax.dot_general(a, b, (dims, ((), ())), preferred_element_type=F32)


def limits(mib):
    return pltpu.CompilerParams(vmem_limit_bytes=mib << 20)


def cost(flops, moved):
    return pl.CostEstimate(flops=flops, bytes_accessed=moved, transcendentals=0)


def enc_grad_kernel(*refs):
    *rows, dz, out = refs
    left = jnp.concatenate([r[0] for r in rows], 0)
    out[0] = dot(left, dz[...], ((0,), (0,))).astype(out.dtype)


def enc_grad_of(rows, dz, blocks):
    layers, size, width = rows[0].shape
    tokens, feats = dz.shape
    block = width // blocks
    return pl.pallas_call(
        enc_grad_kernel,
        grid=(layers, blocks),
        in_specs=[pl.BlockSpec((1, size, block), lambda l, i: (l, 0, i)) for _ in rows]
        + [pl.BlockSpec(dz.shape, lambda l, i: (0, 0))],
        out_specs=pl.BlockSpec((1, block, feats), lambda l, i: (l, i, 0)),
        out_shape=jax.ShapeDtypeStruct((layers, width, feats), BF16),
        compiler_params=limits(24),
        cost_estimate=cost(
            2 * tokens * layers * width * feats, 2 * layers * width * (tokens + feats)
        ),
    )(*rows, dz)


def prep_kernel(table, rows, out):
    _, units, feats, cols = out.shape
    layers = rows.shape[1]
    part = cols // layers
    size = feats * layers
    to = lax.broadcasted_iota(jnp.int32, (size, size), 0)
    at = lax.broadcasted_iota(jnp.int32, (size, size), 1)
    order = jnp.where(at == layers * (to % feats) + to // feats, 1.0, 0.0).astype(BF16)
    flat = rows[...].reshape(size, units * part)
    flat = dot(order, flat, ((1,), (0,))).astype(BF16)
    for u in range(units):
        for layer in range(layers):
            out[0, u, :, layer * part : (layer + 1) * part] = flat[
                layer * feats : (layer + 1) * feats, u * part : (u + 1) * part
            ]


def prep(weight, table, at, count, span, units, room=16):
    feats, layers, _ = weight.shape
    cols = layers * span // units
    return pl.pallas_call(
        prep_kernel,
        grid_spec=pltpu.PrefetchScalarGridSpec(
            num_scalar_prefetch=1,
            grid=(count,),
            in_specs=[
                pl.BlockSpec((feats, layers, span), lambda i, t: (0, 0, t[at + i]))
            ],
            out_specs=pl.BlockSpec((1, units, feats, cols), lambda i, t: (i, 0, 0, 0)),
        ),
        out_shape=jax.ShapeDtypeStruct((count, units, feats, cols), BF16),
        compiler_params=limits(room),
        cost_estimate=cost(0, 4 * count * feats * layers * span),
    )(table, weight)


def place_kernel(count, at, sizes, table, *refs):
    groups, out, sems = refs[:count], refs[-2], refs[-1]
    part = groups[0].shape[3]
    copies = []
    for j, size in enumerate(sizes):
        for i in range(size):
            entry = at + 2 * len(copies)
            start = pl.multiple_of(table[entry] * part, part)
            copy = pltpu.make_async_copy(
                groups[j].at[i], out.at[:, :, pl.ds(start, part)], sems.at[len(copies)]
            )
            copies.append((copy, table[entry + 1] == 1))
    for copy, valid in copies:

        @pl.when(valid)
        def _(copy=copy):
            copy.start()

    for copy, valid in copies:

        @pl.when(valid)
        def _(copy=copy):
            copy.wait()


def place(groups, table, at, shape, held):
    sizes = [g.shape[0] for g in groups]
    body = functools.partial(place_kernel, len(groups), at, sizes)
    operands = list(groups)
    specs = [pl.BlockSpec(memory_space=pltpu.VMEM)] * len(groups)
    aliases = {}
    if held is not None:
        operands.append(held)
        specs.append(pl.BlockSpec(memory_space=pl.ANY))
        aliases = {len(operands): 0}
    return pl.pallas_call(
        body,
        in_specs=[pl.BlockSpec(memory_space=pltpu.SMEM)] + specs,
        out_specs=pl.BlockSpec(memory_space=pl.ANY),
        scratch_shapes=[pltpu.SemaphoreType.DMA((sum(sizes),))],
        out_shape=jax.ShapeDtypeStruct(shape, BF16),
        input_output_aliases=aliases,
        compiler_params=limits(16),
        cost_estimate=cost(0, 4 * sum(g.size for g in groups)),
    )(table, *operands)


def goal_kernel(ends, units, at, table, resid, bias, out):
    layers = resid.shape[1]
    part = resid.shape[2] // units
    for e in range(ends):
        entry = at + 1 + e
        here = pl.ds(pl.multiple_of(table[entry] * part, part), part)
        for layer in range(layers):
            rows = resid[:, layer, here].astype(F32)
            out[0, e, :, layer * part : (layer + 1) * part] = (
                bias[layer, here][None, :] - rows
            )


def goals_of(resid, bias, table, at, chains, ends, units, part):
    tokens, layers, _ = resid.shape
    wide = units // 2 * part

    def block(i, t):
        return t[at] + 2 * i

    return pl.pallas_call(
        functools.partial(goal_kernel, ends, units // 2, at),
        grid_spec=pltpu.PrefetchScalarGridSpec(
            num_scalar_prefetch=1,
            grid=(chains,),
            in_specs=[
                pl.BlockSpec((tokens, layers, wide), lambda i, t: (0, 0, block(i, t))),
                pl.BlockSpec((layers, wide), lambda i, t: (0, block(i, t))),
            ],
            out_specs=pl.BlockSpec(
                (1, ends, tokens, layers * part), lambda i, t: (i, 0, 0, 0)
            ),
        ),
        out_shape=jax.ShapeDtypeStruct((chains, ends, tokens, layers * part), F32),
        compiler_params=limits(24),
        cost_estimate=cost(0, 6 * chains * ends * tokens * layers * part),
    )(table, resid, bias)


def flat_kernel(rows, out):
    layers, count, block = out.shape
    size = count * layers
    to = lax.broadcasted_iota(jnp.int32, (size, size), 0)
    at = lax.broadcasted_iota(jnp.int32, (size, size), 1)
    order = jnp.where(at == layers * (to % count) + to // count, 1.0, 0.0).astype(BF16)
    flat = dot(order, rows[...].reshape(size, block), ((1,), (0,))).astype(BF16)
    for layer in range(layers):
        out[layer] = flat[layer * count : (layer + 1) * count]


def flat_of(resid, piece, pieces, blocks):
    tokens, layers, width = resid.shape
    size, block = tokens // pieces, width // blocks
    return pl.pallas_call(
        flat_kernel,
        grid=(blocks,),
        in_specs=[pl.BlockSpec((size, layers, block), lambda i: (piece, 0, i))],
        out_specs=pl.BlockSpec((layers, size, block), lambda i: (0, 0, i)),
        out_shape=jax.ShapeDtypeStruct((layers, size, width), BF16),
        compiler_params=limits(12),
        cost_estimate=cost(0, 4 * size * layers * width),
    )(resid)


def use_kernel(kinds, n, scale, at, has_sum, table, act_t, *refs):
    m = len(kinds)
    weights, errs, rest = refs[0], refs[1 : n + 1], refs[n + 1 :]
    near, far, total, given = rest[-4:]
    feats, layers, part = near.shape[1:]
    cols = layers * part
    found, added = [], []
    for i, kind in enumerate(kinds):
        entry = at + 3 * i
        e = errs[kind[0]][...]
        for j in kind[1:]:
            e = jnp.where(table[entry] == j, errs[j][...], e)
        found.append(e)
        added.append(e * table[entry + 2].astype(BF16) if 0 in kind[1:] else e)

    def grads(i, e):
        grad = (dot(act_t[...], e, ((1,), (0,))) * scale).astype(BF16)
        for layer in range(layers):
            columns = slice(layer * part, (layer + 1) * part)
            near[i, :, layer, :] = grad[:feats, columns]
            far[i, :, layer, :] = grad[feats:, columns]

    if m == 1:
        grads(0, found[0])
    else:
        given[...] = jnp.concatenate(found, 1)

        def one(i, _):
            grads(i, given[:, pl.ds(pl.multiple_of(i * cols, cols), cols)])
            return 0

        lax.fori_loop(0, m, one, 0)
    e = jnp.concatenate(added, 1)
    w = jnp.concatenate([weights[table[at + 3 * i + 1]] for i in range(m)], 1)
    more = dot(e, w, ((1,), (1,)))
    total[...] = rest[0][...] + more if has_sum else more


def use_of(act_t, weights, errs, total, table, at, kinds, shape, scale):
    feats, layers, _ = shape
    _, double, cols = weights.shape
    tokens = act_t.shape[1]
    m, n = len(kinds), len(errs)
    part = cols // layers

    outs = [
        jax.ShapeDtypeStruct((m, feats, layers, part), BF16),
        jax.ShapeDtypeStruct((m, feats, layers, part), BF16),
        jax.ShapeDtypeStruct((tokens, double), F32),
    ]
    operands = [act_t, weights, *errs]
    if total is not None:
        operands.append(total)
    near_by = pl.BlockSpec(memory_space=pltpu.VMEM)
    return pl.pallas_call(
        functools.partial(use_kernel, kinds, n, scale, at, total is not None),
        in_specs=[pl.BlockSpec(memory_space=pltpu.SMEM)] + [near_by] * len(operands),
        out_specs=[near_by] * 3,
        out_shape=outs,
        scratch_shapes=[pltpu.VMEM((tokens, m * cols), BF16)],
        compiler_params=limits(28),
        cost_estimate=cost(
            4 * m * tokens * double * cols, 2 * m * cols * (tokens + 2 * double)
        ),
    )(table, *operands)


def groups_of(units, steps):
    several = 1 if units == steps + 1 else 2
    groups, now = [[(0, 0)]], []
    for s in range(1, steps + 1):
        now += [(s, -1), (s, 1)] if 2 * s < units else [(s, 0)]
        if s % several == 0 or s == steps:
            groups.append(now)
            now = []
    return groups


def turn_kernel(rows, out):
    out[...] = rows[...].T


def turned(rows):
    return pl.pallas_call(
        turn_kernel,
        out_shape=jax.ShapeDtypeStruct(rows.shape[::-1], rows.dtype),
        compiler_params=limits(12),
        cost_estimate=cost(0, 4 * rows.size),
    )(rows)


def tables(line, ends, units, steps, chains):
    groups = groups_of(units, steps)
    rows = []
    for spot in range(2 * line):
        pos, side = divmod(spot, 2)
        centre = pos + ends - 1

        def taken(s, d):
            if d or not s:
                return d, (centre + d * s) % units, 1
            if centre - s >= 0:
                return -1, centre - s, 1
            if centre + s < units:
                return 1, centre + s, 1
            return 0, centre, 0

        row, at = [], {}

        def add(name, values):
            at[name] = len(row)
            row.extend(values)

        add("prep_a", [(1 - side) * chains])
        add("prep_b", [side * chains])
        add(
            "prep_c",
            [of * chains + k for of in (1 - side, side) for k in range(1, chains)],
        )
        sign = -1 if pos < line // 2 else 1
        block = int(pos >= line // 2)
        add("goals", [2 * side * chains + block])
        add("goals_at", [(centre + sign * e) % (units // 2) for e in range(ends)])
        add("edges", [int(pos in (0, line - 1))] * chains * ends)
        for k in range(chains):
            for i, group in enumerate(groups):
                values = []
                came = sorted({s for s, _ in group if s})
                for s, d in group:
                    way, unit, valid = taken(s, d)
                    src = 0
                    if way:
                        src = 1 + 2 * came.index(s)
                        src += int((way < 0) == (pos % 2 == 0))
                    values += [src, unit, valid]
                add(f"use_{k}_{i}", values)
            values = []
            for group in groups:
                for of in (side, 1 - side):
                    for s, d in group:
                        _, unit, valid = taken(s, d)
                        if d and not 0 <= centre + d * s < units:
                            valid = 0
                        values += [(of * chains + k) * units + unit, valid]
            add(f"place_{k}", values)
        rows.append(row)
    return np.array(rows, np.int32), at


def microstep(resid, enc_weight, enc_bias, dec_weight, dec_bias):
    tokens, _, width = resid.shape
    feats = enc_weight.shape[2]
    scale = 1.0 / math.sqrt(tokens)
    n_cuts = lax.axis_size("cuts")
    bits = n_cuts.bit_length() - 1
    line = lax.axis_size("layer") // 2
    spot = lax.axis_index("layer")
    pos = spot // 2
    cut = lax.axis_index("cuts")
    ups = [(cut >> b) % 2 == 1 for b in range(bits)]
    half = width // 2
    ends = ENDS if half % (128 * (line - 2 + 2 * ENDS)) == 0 else 1
    units = line - 2 + 2 * ends
    steps = line - 2 + ends
    chains = CHAINS
    while chains > 1 and half % (128 * units * chains):
        chains //= 2
    span = half // chains
    part = span // units
    centre = pos + ends - 1
    rows, at = tables(line, ends, units, steps, chains)
    table = lax.dynamic_index_in_dim(jnp.asarray(rows), spot, 0, keepdims=False)

    give = prep(dec_weight, table, at["prep_a"], 1, span, units, 60)
    got = [swap(give[0], "layer", 0)]

    z = dot(resid.reshape(tokens, -1), enc_weight.reshape(-1, feats), ((1,), (0,)))
    held = prep(dec_weight, table, at["prep_b"], 1, span, units)
    own = [held[0]]
    for b in range(bits):
        stay, go = halves(z, ups[b])
        come = swap(go, "cuts", b)
        z = stay + come
    act_mine = jnp.maximum(z + enc_bias[None, :], 0.0).astype(BF16)
    come = swap(act_mine, "layer", 0)
    for k in range(1, chains):
        held = prep(dec_weight, table, at["prep_c"] + k - 1, 1, span, units)
        got.append(swap(held[0], "layer", 0))
        held = prep(dec_weight, table, at["prep_c"] + chains + k - 2, 1, span, units)
        own.append(held[0])
    act = jnp.concatenate([act_mine, come], 1)
    for b in reversed(range(bits)):
        come = swap(act, "cuts", b)
        act = joined(act, come, ups[b])
    goals = goals_of(
        resid, dec_bias, table, at["goals"], chains, ends, units, part
    )

    def exchange(value, ups, downs, even):
        pairs = [
            (2 * i + s, 2 * j + s)
            for i in range(line)
            for j, sources in ((i + 1, ups), (i - 1, downs))
            if i in sources and 0 <= j < line and (i % 2 == 0) == (even == (j > i))
            for s in range(2)
        ]
        if not pairs:
            return None
        return lax.ppermute(value, "layer", pairs)

    def plus(value, more):
        return value if more is None else value + more.astype(F32)

    even = pos % 2 == 0

    both = [
        lax.optimization_barrier(jnp.concatenate([own[k], got[k]], 1))
        for k in range(chains)
    ]
    act_t = turned(act)

    def weights(k, u):
        return lax.dynamic_index_in_dim(both[k], u, 0, keepdims=False)

    def recon(k, u):
        return dot(act, weights(k, u), ((1,), (0,)))

    ahead, behind = [None] * chains, [None] * chains
    errs = [[None] * ends for _ in range(chains)]
    for s in range(1, steps + 1):
        up, down = units - s + pos, s - line + pos
        one = jnp.clip(jnp.where(even, up, down), 0, units - 1)
        two = jnp.clip(jnp.where(even, down, up), 0, units - 1)
        ways = range(0, s), range(line - s, line)
        for k in range(chains):
            give = plus(recon(k, one), behind[k]).astype(BF16)
            first = exchange(give, *ways, True)
            behind_next = None
            if s > 1:
                give = plus(recon(k, two), ahead[k]).astype(BF16)
                behind_next = exchange(give, *ways, False)
            ahead[k], behind[k] = first, behind_next
            late = steps - s
            if late < ends:
                u = jnp.where(pos < line // 2, centre - late, centre + late)
                err = plus(plus(recon(k, u), ahead[k]), behind[k])
                err = err + goals[k, late]
                errs[k][late] = err.astype(BF16)

    dact = dec_grad = None
    grads = [[] for _ in range(chains)]
    groups = groups_of(units, steps)
    ahead = [errs[k][0] for k in range(chains)]
    behind = [errs[k][0] for k in range(chains)]
    came = [[] for _ in range(chains)]

    for s in range(steps + 1):
        ways = range(max(s - ends, 0), line - 1), range(1, line + min(ends - s, 0))
        for k in range(chains if s else 0):
            first = exchange(behind[k], *ways, True)
            second = exchange(ahead[k], *ways, False)
            if 0 < s < ends:
                edge = table[at["edges"] + k * ends + s].astype(BF16)
                second = second + errs[k][s] * edge
            ahead[k], behind[k] = first, second
            came[k] += [first, first if second is None else second]
        for k in range(chains):
            for i, group in enumerate(groups):
                if group[-1][0] != s:
                    continue
                first = sorted({t for t, _ in group if t})
                kinds = [
                    (0,)
                    if not t
                    else tuple(1 + 2 * first.index(t) + j for j in range(2))
                    + (() if d else (0,))
                    for t, d in group
                ]
                near, far, dact = use_of(
                    act_t,
                    both[k],
                    [errs[k][0], *came[k]],
                    dact,
                    table,
                    at[f"use_{k}_{i}"],
                    kinds,
                    dec_weight.shape,
                    scale,
                )
                came[k] = []
                grads[k] += [near, swap(far, "layer", 0)]
    for k in range(chains):
        dec_grad = place(grads[k], table, at[f"place_{k}"], dec_weight.shape, dec_grad)

    flats = []
    for i in range(FLATS):
        flats.append(flat_of(resid, i, FLATS, 4))

    stay, go = halves(dact, ups[0])
    come = swap(go.astype(BF16), "cuts", 0).astype(F32)
    dact = stay + come
    come = swap(dact[:, feats:].astype(BF16), "layer", 0).astype(F32)
    dact = dact[:, :feats] + come
    for b in range(1, bits):
        dact = dact + swap(dact.astype(BF16), "cuts", b).astype(F32)
    live, _ = halves(act[:, :feats], ups[0])
    dz = jnp.where(live > 0, dact * scale, 0.0).astype(BF16)
    come = swap(dz, "cuts", 0)
    dz = joined(dz, come, ups[0])
    enc_grad = enc_grad_of(flats, dz, 2)
    return enc_grad, dec_grad


def solution(mesh):
    placed = (
        P(None, None, "cuts"),
        P(None, "cuts", "layer"),
        P("layer"),
        P("layer", None, "cuts"),
        P(None, "cuts"),
    )
    return jax.shard_map(
        microstep,
        mesh=mesh,
        in_specs=placed,
        out_specs=(P(None, "cuts", "layer"), P("layer", None, "cuts")),
        check_vma=False,
    )
```
